32 devices in a mesh: batch: 4 (over y, x), ctx: 8 (over z, core).
Axes of the slice: x: 2, y: 2, z: 4, core: 2. Of those that a mesh axis runs over, the one named last changes fastest.
Arguments:
- inputs: float32 [4, 1024, 2304], P('batch', 'ctx'), may hold values from -6 to 6
- block_order: int32 [4, 8], P('batch'), may hold values from 0 to 7, each once within a row
- cotangent: float32 [4, 1024, 2304], P('batch', 'ctx'), may hold values from -6 to 6
- attn_gain: bfloat16 [2304], P(('batch', 'ctx')), may hold values from 0.5 to 1.5
- post_attn_gain: bfloat16 [2304], P(('batch', 'ctx')), may hold values from 0.5 to 1.5
- ffn_gain: bfloat16 [2304], P(('batch', 'ctx')), may hold values from 0.5 to 1.5
- post_ffn_gain: bfloat16 [2304], P(('batch', 'ctx')), may hold values from 0.5 to 1.5
- query_weight: bfloat16 [2304, 2048], P(('batch', 'ctx')), may hold values from -0.5 to 0.5
- key_weight: bfloat16 [2304, 1024], P(('batch', 'ctx')), may hold values from -0.125 to 0.125
- value_weight: bfloat16 [2304, 1024], P(('batch', 'ctx')), may hold values from -0.125 to 0.125
- out_weight: bfloat16 [2048, 2304], P(('batch', 'ctx')), may hold values from -0.125 to 0.125
- gate_weight: bfloat16 [9216, 2304], P(('batch', 'ctx')), may hold values from -0.125 to 0.125
- up_weight: bfloat16 [9216, 2304], P(('batch', 'ctx')), may hold values from -0.125 to 0.125
- down_weight: bfloat16 [9216, 2304], P(('batch', 'ctx')), may hold values from -0.0625 to 0.0625
Outputs:
- output: float32 [4, 1024, 2304], P('batch', 'ctx')
- input_grad: float32 [4, 1024, 2304], P('batch', 'ctx')
- query_grad: float32 [2304, 2048], P(('batch', 'ctx'))
- key_grad: float32 [2304, 1024], P(('batch', 'ctx'))
- value_grad: float32 [2304, 1024], P(('batch', 'ctx'))
- out_grad: float32 [2048, 2304], P(('batch', 'ctx'))
- gate_grad: float32 [9216, 2304], P(('batch', 'ctx'))
- up_grad: float32 [9216, 2304], P(('batch', 'ctx'))
- down_grad: float32 [9216, 2304], P(('batch', 'ctx'))
- attn_gain_grad: float32 [2304], P(('batch', 'ctx'))
- post_attn_gain_grad: float32 [2304], P(('batch', 'ctx'))
- ffn_gain_grad: float32 [2304], P(('batch', 'ctx'))
- post_ffn_gain_grad: float32 [2304], P(('batch', 'ctx'))
The draws below stay inside these ranges and needn't reach their ends.
Inputs may be any that keep to these rules, and one draw needn't show every extreme that they name: Each row of block_order names every block of 128 positions of its sequence exactly once.
All inputs are finite; a program needn't handle non-finite values.
Results may differ from the reference program's by a relative error of at most 0.02.
The reference program's roundings to bfloat16 on the way count: a program that leaves them out, or rounds other values in their place, can miss the bound.
Values may be sent and summed in bfloat16 or wider, within the bound.
No kernel may reach another device: no remote copies, remote signals or barrier semaphores. Data moves between devices by JAX's collectives and lax.ppermute only.
A program may use at most 512 MiB of HBM per device.

```python
import math
import jax
import jax.numpy as jnp
from jax import lax

D = 2304
FF = 9216
HEADS = 8
KV_HEADS = 4
HEAD_DIM = 256
TOK_DEV = 128
SEQS = 4
SEQ_LEN = 1024
N_CTX = 8


def strengthened(result, own_key, source, target, shards_of, factor):
    owner, partner = [(jnp.arange(result.shape[dim]) // (result.shape[dim] // shards_of)).reshape([-1 if axis == dim else 1 for axis in range(result.ndim)]) for dim in (source, target)]
    chosen = jax.random.permutation(own_key, shards_of)[partner]
    strong = (owner == chosen) | (owner == (partner + shards_of // 2) % shards_of)
    return jnp.where(strong, factor * result, result)


def levels(rng, extent, shards, low, top_value):
    factor_of, own = 1.0, jax.random.fold_in(rng, 6)
    for axis_at, shards_of in shards:
        heights = jnp.exp(jax.random.uniform(jax.random.fold_in(own, axis_at), (shards_of,), jnp.float32, low / len(shards), top_value / len(shards)))
        factor_of = factor_of * jnp.repeat(heights, extent[axis_at] // shards_of).reshape([-1 if axis == axis_at else 1 for axis in range(len(extent))])
    return factor_of


def bell_draw(key, shape, spread, bound, cuts=(), held_as=jnp.bfloat16):
    values = jax.random.normal(key, shape, jnp.float32) * spread
    if len(cuts) > 0:
        values = levels(key, shape, cuts, -0.22, 0.18) * values
    return jnp.clip(values, min=-bound, max=bound).astype(held_as)


def noise_with(stream_key, extent, spread, most, pieces, heavy, kind=jnp.bfloat16):
    entries = spread * jax.random.normal(stream_key, extent, jnp.float32)
    if pieces:
        entries = entries * levels(stream_key, extent, pieces, -0.22, 0.18)
    return jnp.clip(strengthened(entries, jax.random.fold_in(stream_key, 3), *heavy), -most, most).astype(kind)


def setup_inputs(seed: int = 0) -> dict:
    streams_of = jax.random.split(jax.random.key(seed), 15)
    return {
        "inputs": noise_with(streams_of[0], (SEQS, SEQ_LEN, D), 1.0, 6.0, ((0, 4), (1, 8)), (1, 2, 8, 2.0), jnp.float32),
        "block_order": jax.vmap(lambda own: jax.random.permutation(own, N_CTX))(jax.random.split(streams_of[1], SEQS)).reshape((SEQS, N_CTX)).astype(jnp.int32),
        "cotangent": noise_with(streams_of[2], (SEQS, SEQ_LEN, D), 1.0, 6.0, ((0, 4), (1, 8)), (1, 2, 8, 2.0), jnp.float32),
        "attn_gain": jnp.clip(1.0 + 0.1 * jax.random.normal(streams_of[3], (D,), jnp.float32), 0.5, 1.5).astype(jnp.bfloat16),
        "post_attn_gain": jnp.clip(1.0 + 0.1 * jax.random.normal(streams_of[4], (D,), jnp.float32), 0.5, 1.5).astype(jnp.bfloat16),
        "ffn_gain": jnp.clip(1.0 + 0.1 * jax.random.normal(streams_of[5], (D,), jnp.float32), 0.5, 1.5).astype(jnp.bfloat16),
        "post_ffn_gain": jnp.clip(1.0 + 0.1 * jax.random.normal(streams_of[6], (D,), jnp.float32), 0.5, 1.5).astype(jnp.bfloat16),
        "query_weight": bell_draw(streams_of[7], (D, HEADS * HEAD_DIM), (D // 16) ** -0.5, 0.5, ((0, 32),)),
        "key_weight": bell_draw(streams_of[8], (D, KV_HEADS * HEAD_DIM), D ** -0.5, 0.125, ((0, 32),)),
        "value_weight": bell_draw(streams_of[9], (D, KV_HEADS * HEAD_DIM), D ** -0.5, 0.125, ((0, 32),)),
        "out_weight": bell_draw(streams_of[10], (HEADS * HEAD_DIM, D), (HEADS * HEAD_DIM) ** -0.5, 0.125, ((0, 32),)),
        "gate_weight": bell_draw(streams_of[11], (FF, D), D ** -0.5, 0.125, ((0, 32),)),
        "up_weight": bell_draw(streams_of[12], (FF, D), D ** -0.5, 0.125, ((0, 32),)),
        "down_weight": bell_draw(streams_of[13], (FF, D), FF ** -0.5, 0.0625, ((0, 32),)),
    }


NORM_EPS = 1e-06
SOFT_CAP = 50.0

def normalize(values_in, gain_vec):
    inv_rms = lax.rsqrt(lax.optimization_barrier(jnp.mean(values_in * values_in, axis=-1, keepdims=True)) + NORM_EPS)
    return (values_in * inv_rms * gain_vec.astype(jnp.float32), inv_rms)

def norm_back(values_in, inv_rms, gain_vec, grad_in):
    scaled = values_in * inv_rms
    weighted = grad_in * gain_vec.astype(jnp.float32)
    grad_gain = lax.optimization_barrier(jnp.sum(grad_in * scaled, axis=0))
    grad_values = inv_rms * (weighted - scaled * lax.optimization_barrier(jnp.mean(weighted * scaled, axis=-1, keepdims=True)))
    return (grad_values, grad_gain)

def geglu(gate_val, up_val):
    return jax.nn.gelu(gate_val, approximate=True) * up_val

def rows_product(left_mat, right_mat):
    return lax.dot_general(left_mat, right_mat, (((1,), (1,)), ((), ())), preferred_element_type=jnp.float32)

def cols_product(left_mat, right_mat):
    return lax.dot_general(left_mat, right_mat, (((0,), (0,)), ((), ())), preferred_element_type=jnp.float32)

def round_half(values_in):
    return lax.optimization_barrier(values_in.astype(jnp.bfloat16)).astype(jnp.float32)

def one_sequence(rows_x, grad_y, block_row, params):
    gain_one, gain_two, gain_three, gain_four, w_query, w_key, w_value, w_out, w_gate, w_up, w_down = params
    length = rows_x.shape[0]
    groups = KV_HEADS
    ratio = HEADS // KV_HEADS
    scale = 1.0 / math.sqrt(HEAD_DIM)
    row_index = jnp.arange(length, dtype=jnp.int32)
    position = block_row[row_index // TOK_DEV].astype(jnp.int32) * TOK_DEV + row_index % TOK_DEV
    visible = position[None, :] <= position[:, None]
    normed, inv_one = normalize(rows_x, gain_one)
    normed_in = normed.astype(jnp.bfloat16)
    query = jnp.dot(normed_in, w_query, preferred_element_type=jnp.float32).astype(jnp.bfloat16)
    keys = jnp.dot(normed_in, w_key, preferred_element_type=jnp.float32).astype(jnp.bfloat16)
    values = jnp.dot(normed_in, w_value, preferred_element_type=jnp.float32).astype(jnp.bfloat16)
    q_heads = query.reshape(length, groups, ratio, HEAD_DIM).astype(jnp.float32)
    k_heads = keys.reshape(length, groups, HEAD_DIM).astype(jnp.float32)
    v_heads = values.reshape(length, groups, HEAD_DIM).astype(jnp.float32)
    tanh_val = jnp.tanh(jnp.einsum('tgrd,jgd->grtj', q_heads, k_heads) * scale / SOFT_CAP)
    capped = SOFT_CAP * tanh_val
    raw = jnp.where(visible, jnp.exp(capped), 0.0)
    total = lax.optimization_barrier(jnp.sum(raw, axis=3))
    accum = jnp.einsum('grtj,jgd->tgrd', round_half(raw), v_heads)
    attended = (accum / jnp.transpose(total, (2, 0, 1))[..., None]).reshape(length, HEADS * HEAD_DIM).astype(jnp.bfloat16)
    branch = jnp.dot(attended, w_out, preferred_element_type=jnp.float32)
    branch_normed, inv_two = normalize(branch, gain_two)
    middle = rows_x + branch_normed
    normed_m, inv_three = normalize(middle, gain_three)
    normed_mid = normed_m.astype(jnp.bfloat16)
    gate_act = rows_product(normed_mid, w_gate)
    up_act = rows_product(normed_mid, w_up)
    hidden_f, pull_back = jax.vjp(geglu, gate_act, up_act)
    hidden = hidden_f.astype(jnp.bfloat16)
    ffn_out = jnp.dot(hidden, w_down, preferred_element_type=jnp.float32)
    ffn_normed, inv_four = normalize(ffn_out, gain_four)
    output = middle + ffn_normed
    grad_ffn, grad_four = norm_back(ffn_out, inv_four, gain_four, grad_y)
    grad_ffn_b = grad_ffn.astype(jnp.bfloat16)
    grad_hidden = rows_product(grad_ffn_b, w_down)
    grad_gate, grad_up = pull_back(grad_hidden)
    grad_gate_b = grad_gate.astype(jnp.bfloat16)
    grad_up_b = grad_up.astype(jnp.bfloat16)
    down_term = cols_product(hidden, grad_ffn_b)
    gate_term = cols_product(grad_gate_b, normed_mid)
    up_term = cols_product(grad_up_b, normed_mid)
    grad_nm = jnp.dot(grad_gate_b, w_gate, preferred_element_type=jnp.float32) + jnp.dot(grad_up_b, w_up, preferred_element_type=jnp.float32)
    grad_mid_part, grad_three = norm_back(middle, inv_three, gain_three, grad_nm)
    grad_mid = grad_y + grad_mid_part
    grad_branch, grad_two = norm_back(branch, inv_two, gain_two, grad_mid)
    grad_branch_b = grad_branch.astype(jnp.bfloat16)
    out_term = cols_product(attended, grad_branch_b)
    grad_att = rows_product(grad_branch_b, w_out).astype(jnp.bfloat16)
    ga_heads = grad_att.reshape(length, groups, ratio, HEAD_DIM).astype(jnp.float32)
    at_heads = attended.reshape(length, groups, ratio, HEAD_DIM).astype(jnp.float32)
    delta = jnp.transpose(lax.optimization_barrier(jnp.sum(ga_heads * at_heads, axis=3)), (1, 2, 0))
    prob = jnp.where(visible, jnp.exp(capped) / total[..., None], 0.0)
    dprob = jnp.einsum('tgrd,jgd->grtj', ga_heads, v_heads)
    grad_z = round_half(prob * (dprob - delta[..., None]) * (1.0 - tanh_val * tanh_val) * scale)
    grad_query = jnp.einsum('grtj,jgd->tgrd', grad_z, k_heads).reshape(length, HEADS * HEAD_DIM).astype(jnp.bfloat16)
    grad_keys = jnp.einsum('grtj,tgrd->jgd', grad_z, q_heads).reshape(length, KV_HEADS * HEAD_DIM).astype(jnp.bfloat16)
    grad_values = jnp.einsum('grtj,tgrd->jgd', round_half(prob), ga_heads).reshape(length, KV_HEADS * HEAD_DIM).astype(jnp.bfloat16)
    query_term = cols_product(normed_in, grad_query)
    key_term = cols_product(normed_in, grad_keys)
    value_term = cols_product(normed_in, grad_values)
    grad_in = rows_product(grad_query, w_query) + rows_product(grad_keys, w_key) + rows_product(grad_values, w_value)
    grad_x_part, grad_one = norm_back(rows_x, inv_one, gain_one, grad_in)
    input_grad = grad_mid + grad_x_part
    terms = (query_term, key_term, value_term, out_term, gate_term, up_term, down_term, grad_one, grad_two, grad_three, grad_four)
    return (output, input_grad, terms)

def add_terms(first_val, second_val):
    return first_val + second_val

def reference(inputs, block_order, cotangent, attn_gain, post_attn_gain, ffn_gain, post_ffn_gain, query_weight, key_weight, value_weight, out_weight, gate_weight, up_weight, down_weight):
    params = (attn_gain, post_attn_gain, ffn_gain, post_ffn_gain, query_weight, key_weight, value_weight, out_weight, gate_weight, up_weight, down_weight)

    def per_sequence(carried, item_in):
        rows_x, grad_y, block_row = item_in
        output, input_grad, terms = one_sequence(rows_x, grad_y, block_row, params)
        return (jax.tree.map(add_terms, carried, terms), (output, input_grad))
    starting = (jnp.zeros((D, HEADS * HEAD_DIM), jnp.float32), jnp.zeros((D, KV_HEADS * HEAD_DIM), jnp.float32), jnp.zeros((D, KV_HEADS * HEAD_DIM), jnp.float32), jnp.zeros((HEADS * HEAD_DIM, D), jnp.float32), jnp.zeros((FF, D), jnp.float32), jnp.zeros((FF, D), jnp.float32), jnp.zeros((FF, D), jnp.float32), jnp.zeros((D,), jnp.float32), jnp.zeros((D,), jnp.float32), jnp.zeros((D,), jnp.float32), jnp.zeros((D,), jnp.float32))
    totals, stacked = lax.scan(per_sequence, starting, (inputs, cotangent, block_order))
    outputs, input_grads = stacked
    query_grad, key_grad, value_grad, out_grad, gate_grad, up_grad, down_grad, attn_gain_grad, post_attn_gain_grad, ffn_gain_grad, post_ffn_gain_grad = totals
    return (outputs, input_grads, query_grad, key_grad, value_grad, out_grad, gate_grad, up_grad, down_grad, attn_gain_grad, post_attn_gain_grad, ffn_gain_grad, post_ffn_gain_grad)
```

```python
import functools
import math

import jax
import jax.numpy as jnp
from jax import lax
from jax.sharding import PartitionSpec as P


HEADS = 8
KV_HEADS = 4
HEAD_DIM = 256

NORM_EPS = 1e-06
SOFT_CAP = 50.0

BF16 = jnp.bfloat16
F32 = jnp.float32


def normalize(values_in, gain_vec):
    inv_rms = lax.rsqrt(jnp.mean(values_in * values_in, axis=-1, keepdims=True) + NORM_EPS)
    return (values_in * inv_rms * gain_vec.astype(F32), inv_rms)


def norm_back(values_in, inv_rms, gain_vec, grad_in):
    scaled = values_in * inv_rms
    weighted = grad_in * gain_vec.astype(F32)
    grad_gain = jnp.sum(grad_in * scaled, axis=0)
    grad_values = inv_rms * (
        weighted - scaled * jnp.mean(weighted * scaled, axis=-1, keepdims=True)
    )
    return (grad_values, grad_gain)


def geglu(gate_val, up_val):
    return jax.nn.gelu(gate_val, approximate=True) * up_val


def product(left_mat, right_mat):
    return jnp.dot(left_mat, right_mat, preferred_element_type=F32)


def rows_product(left_mat, right_mat):
    return lax.dot_general(
        left_mat, right_mat, (((1,), (1,)), ((), ())), preferred_element_type=F32
    )


def cols_product(left_mat, right_mat):
    return lax.dot_general(
        left_mat, right_mat, (((0,), (0,)), ((), ())), preferred_element_type=F32
    )


class Line:
    def __init__(self, ctx_size):
        self.size = ctx_size // 2
        self.index = lax.axis_index("ctx")
        self.at = self.index // 2
        self.parity = self.index % 2
        self.sources = []
        for z in range(self.size):
            first = 1 if z < self.size / 2 else -1
            reach = [d for k in range(1, self.size) for d in (k * first, -k * first)]
            self.sources.append([0] + [d for d in reach if 0 <= z + d < self.size])

    def move(self, rows, step, froms):
        pairs = [(2 * z + p, 2 * (z + step) + p) for z in froms for p in range(2)]
        return lax.ppermute(rows, "ctx", pairs)

    def partner(self, rows):
        return lax.ppermute(rows, "ctx", [(c, c ^ 1) for c in range(2 * self.size)])

    def pick(self, options):
        known = [o for o in options if o is not None]
        result = known[0]
        for other in {id(o): o for o in known[1:] if o is not known[0]}.values():
            places = [z for z, o in enumerate(options) if o is other]
            here = self.at == places[0]
            for z in places[1:]:
                here = here | (self.at == z)
            result = jnp.where(here, other, result)
        return result

    def gather(self, rows, work=None):
        arrived, slots, results = {0: rows}, [rows], []
        for k in range(1, self.size):
            arrived[-k] = self.move(arrived[1 - k], 1, range(k - 1, self.size - 1))
            arrived[k] = self.move(arrived[k - 1], -1, range(1, self.size - k + 1))
            if work is not None:
                results.append(work(k, slots))
            slots.append(
                self.pick([arrived[self.sources[z][k]] for z in range(self.size)])
            )
        return slots, results

    def part_for(self, parts, distance):
        return self.pick(
            [
                parts[self.sources[z].index(distance)] if distance in self.sources[z] else None
                for z in range(self.size)
            ]
        )

    def scatter(self, parts, work=()):
        upward = downward = 0.0
        results = []
        for step, k in enumerate(range(self.size - 1, 0, -1), 1):
            upward = (self.part_for(parts, k) + upward).astype(BF16)
            downward = (self.part_for(parts, -k) + downward).astype(BF16)
            if step <= len(work):
                function, given = work[step - 1]
                upward, downward, given = lax.optimization_barrier((upward, downward, given))
            upward = self.move(upward, 1, range(self.size - k)).astype(F32)
            downward = self.move(downward, -1, range(k, self.size)).astype(F32)
            if step <= len(work):
                results.append(function(*given))
        return parts[0] + upward + downward, results

    def shift(self, rows, k):
        pairs = [
            (2 * ((z + k) % self.size) + p, 2 * z + p) for z in range(self.size) for p in range(2)
        ]
        return lax.ppermute(rows, "ctx", pairs)

    def slot_blocks(self, block_row, parity):
        table = [[z + d for d in self.sources[z]] for z in range(self.size)]
        positions = lax.dynamic_index_in_dim(
            jnp.asarray(table, jnp.int32), self.at, axis=0, keepdims=False
        )
        ids = jnp.arange(block_row.shape[0], dtype=jnp.int32)
        matches = ids[None, :] == (2 * positions + parity)[:, None]
        return jnp.sum(jnp.where(matches, block_row[None, :], 0), axis=1)


def across(rows, bit, batch_size):
    return lax.ppermute(rows, "batch", [(b, b ^ bit) for b in range(batch_size)])


def cube_order(bits):
    order = [0]
    for bit in bits:
        order = order + [mask ^ bit for mask in order]
    return order


def cube_gather(rows, bits, batch_size):
    pieces = [rows]
    for bit in bits:
        more = []
        for piece in pieces:
            more.append(across(piece, bit, batch_size))
        pieces = pieces + more
    return [pieces[cube_order(bits).index(k)] for k in range(batch_size)]


def batch_scatter(pieces, batch_index, batch_size):
    def piece(k):
        return lax.dynamic_index_in_dim(pieces, batch_index ^ k, axis=0, keepdims=False)

    total = piece(0).astype(F32)
    received = [across(piece(k), k, batch_size) for k in range(1, batch_size)]
    return sum((one.astype(F32) for one in received), total)


def cube_send(pieces, bit, batch_size):
    half = len(pieces) // 2
    return [across(piece.astype(BF16), bit, batch_size) for piece in pieces[half:]]


def cube_add(pieces, sent):
    half = len(pieces) // 2
    return [own.astype(F32) + other.astype(F32) for own, other in zip(pieces[:half], sent)]


def everywhere(array, line, batch_size):
    array = sum((line.shift(array, k) for k in range(1, line.size)), array)
    array = sum((across(array, k, batch_size) for k in range(1, batch_size)), array)
    return array + line.partner(array)


def on_device(
    sizes,
    inputs,
    block_order,
    cotangent,
    attn_gain,
    post_attn_gain,
    ffn_gain,
    post_ffn_gain,
    query_weight,
    key_weight,
    value_weight,
    out_weight,
    gate_weight,
    up_weight,
    down_weight,
):
    batch_size, ctx_size = sizes
    line = Line(ctx_size)
    devices = batch_size * ctx_size
    flat_index = lax.axis_index("batch") * ctx_size + line.index
    local_rows = inputs.shape[1]
    features = inputs.shape[2]
    rows_x = inputs.reshape(local_rows, features)
    grad_y = cotangent.reshape(local_rows, features)
    block_row = block_order.reshape(-1)
    scale = 1.0 / math.sqrt(HEAD_DIM)
    line_rows = local_rows * line.size
    heads = HEADS // line.size
    sharing = line.size // KV_HEADS
    query_width = heads * HEAD_DIM
    bits_up = [1 << i for i in range(batch_size.bit_length() - 1)]
    bits_down = bits_up[::-1]
    owner_pairs = [
        (c * batch_size + b, b * ctx_size + c) for b in range(batch_size) for c in range(ctx_size)
    ]

    def slots(rows):
        return [
            rows[slot * local_rows : (slot + 1) * local_rows] for slot in range(line.size)
        ]

    def stack(parts):
        return jnp.concatenate(parts, axis=0)

    own_gains = jnp.stack((attn_gain, post_attn_gain, ffn_gain, post_ffn_gain))
    piece = own_gains.shape[1]
    spread = lax.dynamic_update_slice(
        jnp.zeros((4, devices, piece), BF16), own_gains[:, None], (0, flat_index, 0)
    )
    gains = everywhere(spread, line, batch_size).reshape(4, features)
    gain_one, gain_two, gain_three, gain_four = gains[0], gains[1], gains[2], gains[3]

    weight_rows = query_weight.shape[0]

    def kv_targets(weight):
        return jnp.repeat(weight.reshape(weight_rows, KV_HEADS, HEAD_DIM), sharing, axis=1)

    def from_here(stacked):
        return lax.dynamic_slice_in_dim(
            jnp.concatenate((stacked, stacked), axis=0), line.at, line.size, axis=0
        )

    def from_start(turned):
        return lax.dynamic_slice_in_dim(
            jnp.concatenate((turned, turned), axis=0),
            (line.size - line.at) % line.size,
            line.size,
            axis=0,
        )

    per_target = jnp.concatenate(
        (
            query_weight.reshape(weight_rows, line.size, query_width),
            kv_targets(key_weight),
            kv_targets(value_weight),
        ),
        axis=2,
    )
    turned = from_here(jnp.transpose(per_target, (1, 0, 2)))
    received = [turned[0]] + [
        line.shift(turned[line.size - k], k) for k in range(1, line.size)
    ]
    batch_index = lax.axis_index("batch")
    even = line.parity == 0

    def placed(pieces, shape, block):
        whole = jnp.zeros(shape, BF16)
        for k, one in enumerate(pieces):
            for parity, rows in ((line.parity, one), (1 - line.parity, line.partner(one))):
                start, update = block(batch_index ^ k, parity, rows)
                whole = lax.dynamic_update_slice(whole, update, start)
        return whole

    w_half = from_start(jnp.stack(received))
    pieces = cube_gather(w_half, bits_up, batch_size)
    w_qkv = placed(
        pieces,
        (batch_size, line.size, 2) + w_half.shape[1:],
        lambda b, parity, rows: ((b, 0, parity, 0, 0), rows[None, :, None]),
    ).reshape(features, query_width + 2 * HEAD_DIM)

    out_half = lax.ppermute(out_weight, ("batch", "ctx"), owner_pairs)
    out_pieces = cube_gather(out_half, bits_up, batch_size)
    w_out = placed(
        out_pieces,
        (2, batch_size) + out_half.shape,
        lambda b, parity, rows: ((parity, b, 0, 0), rows[None, None]),
    ).reshape(-1, features)

    unit_rows = gate_weight.shape[0]
    gate_pieces = cube_gather(gate_weight, bits_up, batch_size)
    up_pieces = cube_gather(up_weight, bits_down, batch_size)
    down_pieces = cube_gather(down_weight, bits_up, batch_size)

    normed, inv_one = normalize(rows_x, gain_one)
    normed_in, _ = line.gather(normed.astype(BF16))
    qkv = stack([product(rows, w_qkv).astype(BF16) for rows in normed_in])
    own_kv = qkv[:, query_width:]
    kv = stack((own_kv, line.partner(own_kv)))
    keys = kv[:, :HEAD_DIM]
    values = kv[:, HEAD_DIM:]

    def by_head(rows):
        return stack([rows[:, h * HEAD_DIM : (h + 1) * HEAD_DIM] for h in range(heads)])

    def by_row(stacked):
        return jnp.concatenate(
            [stacked[h * line_rows : (h + 1) * line_rows] for h in range(heads)], axis=1
        )

    query = by_head(qkv[:, :query_width])

    def row_positions(blocks):
        inside = jnp.arange(local_rows, dtype=jnp.int32)
        return (blocks[:, None] * local_rows + inside[None, :]).reshape(-1)

    query_pos = row_positions(line.slot_blocks(block_row, line.parity))
    key_pos = jnp.concatenate(
        (query_pos, row_positions(line.slot_blocks(block_row, 1 - line.parity)))
    )
    visible = key_pos[None, :] <= jnp.tile(query_pos, heads)[:, None]
    tanh_val = jnp.tanh(rows_product(query, keys) * scale / SOFT_CAP)
    raw = jnp.where(visible, jnp.exp(SOFT_CAP * tanh_val), 0.0)
    totals = jnp.sum(raw, axis=1, keepdims=True)
    attended = (product(raw.astype(BF16), values) / totals).astype(BF16)
    attended_rows = by_row(attended)
    branch, _ = line.scatter(slots(product(attended_rows, w_out)))
    branch_normed, inv_two = normalize(branch, gain_two)
    middle = rows_x + branch_normed
    normed_m, inv_three = normalize(middle, gain_three)

    def with_partner(rows):
        return stack((rows, line.partner(rows)))

    def pair_sum(part):
        other = line.partner(part[local_rows:].astype(BF16))
        return part[:local_rows] + other.astype(F32)

    def expand(rows):
        both = with_partner(rows)
        gate_act = rows_product(both, w_gate)
        up_act = rows_product(both, w_up)
        return both, gate_act, up_act, geglu(gate_act, up_act).astype(BF16)

    def contract(forward):
        return pair_sum(product(forward[3], w_down))

    expanded, parts = [], []

    w_gate, w_up = stack(gate_pieces), stack(up_pieces)
    w_down = stack(down_pieces)

    def forward_work(k, arrived):
        expanded.append(expand(arrived[k - 1]))
        if k > 1:
            parts.append(contract(expanded[k - 2]))

    normed_rows, _ = line.gather(normed_m.astype(BF16), forward_work)
    expanded.append(expand(normed_rows[-1]))
    last = contract(expanded[-1])
    parts = parts + [contract(expanded[-2]), last]
    mid_rows = stack([e[0] for e in expanded])
    ffn_out, _ = line.scatter(parts)
    ffn_normed, inv_four = normalize(ffn_out, gain_four)
    output = middle + ffn_normed

    grad_ffn, grad_four = norm_back(ffn_out, inv_four, gain_four, grad_y)

    def shrink(rows, forward):
        both = with_partner(rows)
        _, pull_back = jax.vjp(geglu, forward[1], forward[2])
        gate_part, up_part = pull_back(rows_product(both, w_down))
        gate_part, up_part = gate_part.astype(BF16), up_part.astype(BF16)
        part = product(gate_part, w_gate) + product(up_part, w_up)
        return both, gate_part, up_part, pair_sum(part)

    ffn_rows, results = line.gather(
        grad_ffn.astype(BF16), lambda k, arrived: shrink(arrived[k - 1], expanded[k - 1])
    )
    shrunk = list(results) + [shrink(ffn_rows[-1], expanded[-1])]
    ffn_rows = stack([e[0] for e in shrunk])
    hidden = stack([e[3] for e in expanded])
    grad_gate = stack([e[1] for e in shrunk])
    grad_up = stack([e[2] for e in shrunk])

    def unit_grads(left, right, bits):
        total = cols_product(left, right).astype(BF16)
        pieces = [total[i * unit_rows : (i + 1) * unit_rows] for i in cube_order(bits)]
        return pieces, cube_send(pieces, bits[-1], batch_size)

    def first_sum(pieces, sent, bits):
        pieces = cube_add(pieces, sent)
        if len(bits) == 1:
            return pieces, None
        return pieces, cube_send(pieces, bits[-2], batch_size)

    def rest(pieces, sent, bits):
        for bit in reversed(bits[:-1]):
            sent = cube_send(pieces, bit, batch_size) if sent is None else sent
            pieces, sent = cube_add(pieces, sent), None
        return pieces[0]

    grad_nm, (down_sum, gate_sum, up_sum) = line.scatter(
        [e[3] for e in shrunk],
        (
            (functools.partial(unit_grads, bits=bits_up), (hidden, ffn_rows)),
            (functools.partial(unit_grads, bits=bits_down), (grad_gate, mid_rows)),
            (functools.partial(unit_grads, bits=bits_up), (grad_up, mid_rows)),
        ),
    )

    grad_mid_part, grad_three = norm_back(middle, inv_three, gain_three, grad_nm)
    grad_mid = grad_y + grad_mid_part
    grad_branch, grad_two = norm_back(branch, inv_two, gain_two, grad_mid)
    gain_grads = jnp.stack((grad_two, grad_three, grad_four))

    gain_grads = everywhere(gain_grads, line, batch_size)
    gain_grads = lax.dynamic_slice_in_dim(gain_grads, flat_index * piece, piece, axis=1)

    def back_work(k, arrived):
        if k == line.size - 2:
            return first_sum(*down_sum, bits_up)
        if k == line.size - 1:
            return first_sum(*gate_sum, bits_down)

    branch_rows, back_results = line.gather(grad_branch.astype(BF16), back_work)
    grad_branch_b = stack(branch_rows)
    down_grad = rest(*back_results[-2], bits_up)
    gate_grad = rest(*back_results[-1], bits_down)
    grad_att = by_head(rows_product(grad_branch_b, w_out).astype(BF16))
    delta = jnp.sum(grad_att.astype(F32) * attended.astype(F32), axis=1, keepdims=True)
    prob = raw / totals
    dprob = rows_product(grad_att, values)
    grad_z = (prob * (dprob - delta) * (1.0 - tanh_val * tanh_val) * scale).astype(BF16)
    grad_query = by_row(product(grad_z, keys).astype(BF16))
    grad_kv = jnp.concatenate(
        (cols_product(grad_z, query), cols_product(prob.astype(BF16), grad_att)), axis=1
    )
    grad_kv = grad_kv[:line_rows] + line.partner(grad_kv[line_rows:])
    grad_qkv = jnp.concatenate((grad_query, grad_kv.astype(BF16)), axis=1)

    def qkv_work(rows, grads):
        part = cols_product(rows, grads).astype(BF16).reshape(
            batch_size, line.size, 2, weight_rows, -1
        )
        part_even, part_odd = part[:, :, 0], part[:, :, 1]
        other = line.partner(jnp.where(even, part_odd, part_even))
        return jnp.where(even, part_even, part_odd), other

    grad_in, (qkv_parts, up_sum) = line.scatter(
        slots(rows_product(grad_qkv, w_qkv)),
        (
            (qkv_work, (stack(normed_in), grad_qkv)),
            (lambda: first_sum(*up_sum, bits_up), ()),
        ),
    )
    up_grad = rest(*up_sum, bits_up)
    qkv_part = (qkv_parts[0].astype(F32) + qkv_parts[1].astype(F32)).astype(BF16)

    out_part = cols_product(attended_rows, grad_branch_b).reshape(2, -1, features)
    out_other = line.partner(jnp.where(even, out_part[1], out_part[0]).astype(BF16))
    out_part = jnp.where(even, out_part[0], out_part[1]) + out_other.astype(F32)
    out_part = batch_scatter(
        out_part.astype(BF16).reshape(batch_size, -1, features), batch_index, batch_size
    )
    out_grad = lax.ppermute(
        out_part.astype(BF16), ("batch", "ctx"), [(there, here) for here, there in owner_pairs]
    ).astype(F32)

    qkv_part = batch_scatter(qkv_part, batch_index, batch_size)
    turned = from_here(qkv_part.astype(BF16))
    returned = [turned[0]] + [
        line.shift(turned[line.size - k], k) for k in range(1, line.size)
    ]
    returned = from_start(jnp.stack(returned)).astype(F32)

    def columns(part):
        return jnp.transpose(part, (1, 0, 2)).reshape(weight_rows, -1)

    def kv_columns(part):
        part = part.reshape(KV_HEADS, sharing, weight_rows, HEAD_DIM)
        return columns(jnp.sum(part, axis=1))

    query_grad = columns(returned[:, :, :query_width])
    key_grad = kv_columns(returned[:, :, query_width : query_width + HEAD_DIM])
    value_grad = kv_columns(returned[:, :, query_width + HEAD_DIM :])

    grad_x_part, _ = norm_back(rows_x, inv_one, gain_one, grad_in)
    input_grad = grad_mid + grad_x_part
    attn_gain_grad = (
        jnp.sum(query_weight.astype(F32) * query_grad, axis=1)
        + jnp.sum(key_weight.astype(F32) * key_grad, axis=1)
        + jnp.sum(value_weight.astype(F32) * value_grad, axis=1)
    ) / attn_gain.astype(F32)
    return (
        output.reshape(1, local_rows, features),
        input_grad.reshape(1, local_rows, features),
        query_grad,
        key_grad,
        value_grad,
        out_grad,
        gate_grad,
        up_grad,
        down_grad,
        attn_gain_grad,
        gain_grads[0],
        gain_grads[1],
        gain_grads[2],
    )


def solution(mesh):
    sizes = (mesh.shape["batch"], mesh.shape["ctx"])
    rows = P("batch", "ctx", None)
    owned = P(("batch", "ctx"), None)
    vector = P(("batch", "ctx"))

    def program(*args):
        return on_device(sizes, *args)

    return jax.shard_map(
        program,
        mesh=mesh,
        in_specs=(rows, P("batch", None), rows) + (vector,) * 4 + (owned,) * 7,
        out_specs=(rows, rows) + (owned,) * 7 + (vector,) * 4,
        check_vma=False,
    )
```

```python
import functools
import math

import jax
import jax.numpy as jnp
from jax import lax
from jax.sharding import PartitionSpec as P


HEADS = 8
KV_HEADS = 4
HEAD_DIM = 256

NORM_EPS = 1e-06
SOFT_CAP = 50.0

BF16 = jnp.bfloat16
F32 = jnp.float32


def normalize(values_in, gain_vec):
    inv_rms = lax.rsqrt(jnp.mean(values_in * values_in, axis=-1, keepdims=True) + NORM_EPS)
    return (values_in * inv_rms * gain_vec.astype(F32), inv_rms)


def norm_back(values_in, inv_rms, gain_vec, grad_in):
    scaled = values_in * inv_rms
    weighted = grad_in * gain_vec.astype(F32)
    grad_gain = jnp.sum(grad_in * scaled, axis=0)
    grad_values = inv_rms * (
        weighted - scaled * jnp.mean(weighted * scaled, axis=-1, keepdims=True)
    )
    return (grad_values, grad_gain)


def geglu(gate_val, up_val):
    return jax.nn.gelu(gate_val, approximate=True) * up_val


def product(left_mat, right_mat):
    return jnp.dot(left_mat, right_mat, preferred_element_type=F32)


def rows_product(left_mat, right_mat):
    return lax.dot_general(
        left_mat, right_mat, (((1,), (1,)), ((), ())), preferred_element_type=F32
    )


def cols_product(left_mat, right_mat):
    return lax.dot_general(
        left_mat, right_mat, (((0,), (0,)), ((), ())), preferred_element_type=F32
    )


class Line:
    def __init__(self, ctx_size):
        self.size = ctx_size // 2
        self.index = lax.axis_index("ctx")
        self.at = self.index // 2
        self.parity = self.index % 2
        self.sources = []
        for z in range(self.size):
            first = 1 if z < self.size / 2 else -1
            reach = [d for k in range(1, self.size) for d in (k * first, -k * first)]
            self.sources.append([0] + [d for d in reach if 0 <= z + d < self.size])

    def move(self, rows, step, froms):
        pairs = [(2 * z + p, 2 * (z + step) + p) for z in froms for p in range(2)]
        return lax.ppermute(rows, "ctx", pairs)

    def partner(self, rows):
        return lax.ppermute(rows, "ctx", [(c, c ^ 1) for c in range(2 * self.size)])

    def pick(self, options):
        known = [o for o in options if o is not None]
        result = known[0]
        for other in {id(o): o for o in known[1:] if o is not known[0]}.values():
            places = [z for z, o in enumerate(options) if o is other]
            here = self.at == places[0]
            for z in places[1:]:
                here = here | (self.at == z)
            result = jnp.where(here, other, result)
        return result

    def gather(self, rows, work=None):
        arrived, slots, results = {0: rows}, [rows], []
        for k in range(1, self.size):
            arrived[-k] = self.move(arrived[1 - k], 1, range(k - 1, self.size - 1))
            arrived[k] = self.move(arrived[k - 1], -1, range(1, self.size - k + 1))
            if work is not None:
                results.append(work(k, slots))
            slots.append(
                self.pick([arrived[self.sources[z][k]] for z in range(self.size)])
            )
        return slots, results

    def part_for(self, parts, distance):
        return self.pick(
            [
                parts[self.sources[z].index(distance)] if distance in self.sources[z] else None
                for z in range(self.size)
            ]
        )

    def scatter(self, parts, work=()):
        upward = downward = 0.0
        results = []
        for step, k in enumerate(range(self.size - 1, 0, -1), 1):
            upward = (self.part_for(parts, k) + upward).astype(BF16)
            downward = (self.part_for(parts, -k) + downward).astype(BF16)
            if step <= len(work):
                function, given = work[step - 1]
                upward, downward, given = lax.optimization_barrier((upward, downward, given))
            upward = self.move(upward, 1, range(self.size - k)).astype(F32)
            downward = self.move(downward, -1, range(k, self.size)).astype(F32)
            if step <= len(work):
                results.append(function(*given))
        return parts[0] + upward + downward, results

    def shift(self, rows, k):
        pairs = [
            (2 * ((z + k) % self.size) + p, 2 * z + p) for z in range(self.size) for p in range(2)
        ]
        return lax.ppermute(rows, "ctx", pairs)

    def slot_blocks(self, block_row, parity):
        table = [[z + d for d in self.sources[z]] for z in range(self.size)]
        positions = lax.dynamic_index_in_dim(
            jnp.asarray(table, jnp.int32), self.at, axis=0, keepdims=False
        )
        ids = jnp.arange(block_row.shape[0], dtype=jnp.int32)
        matches = ids[None, :] == (2 * positions + parity)[:, None]
        return jnp.sum(jnp.where(matches, block_row[None, :], 0), axis=1)


def across(rows, bit, batch_size):
    return lax.ppermute(rows, "batch", [(b, b ^ bit) for b in range(batch_size)])


def cube_order(bits):
    order = [0]
    for bit in bits:
        order = order + [mask ^ bit for mask in order]
    return order


def cube_gather(rows, bits, batch_size):
    pieces = [rows]
    for bit in bits:
        more = []
        for piece in pieces:
            more.append(across(piece, bit, batch_size))
        pieces = pieces + more
    return [pieces[cube_order(bits).index(k)] for k in range(batch_size)]


def batch_scatter(pieces, batch_index, batch_size):
    def piece(k):
        return lax.dynamic_index_in_dim(pieces, batch_index ^ k, axis=0, keepdims=False)

    total = piece(0).astype(F32)
    received = [across(piece(k), k, batch_size) for k in range(1, batch_size)]
    return sum((one.astype(F32) for one in received), total)


def cube_send(pieces, bit, batch_size):
    half = len(pieces) // 2
    return [across(piece.astype(BF16), bit, batch_size) for piece in pieces[half:]]


def cube_add(pieces, sent):
    half = len(pieces) // 2
    return [own.astype(F32) + other.astype(F32) for own, other in zip(pieces[:half], sent)]


def everywhere(array, line, batch_size, rounds):
    for one in rounds:
        if one == "line":
            sent = [line.shift(array, k) for k in range(1, line.size)]
        elif one == "batch":
            sent = [across(array, k, batch_size) for k in range(1, batch_size)]
        else:
            sent = [line.partner(array)]
        array = sum(sent, array)
    return array


def batch_pieces(rows, batch_size):
    return [rows] + [across(rows, k, batch_size) for k in range(1, batch_size)]


def on_device(
    sizes,
    inputs,
    block_order,
    cotangent,
    attn_gain,
    post_attn_gain,
    ffn_gain,
    post_ffn_gain,
    query_weight,
    key_weight,
    value_weight,
    out_weight,
    gate_weight,
    up_weight,
    down_weight,
):
    batch_size, ctx_size = sizes
    line = Line(ctx_size)
    devices = batch_size * ctx_size
    flat_index = lax.axis_index("batch") * ctx_size + line.index
    local_rows = inputs.shape[1]
    features = inputs.shape[2]
    rows_x = inputs.reshape(local_rows, features)
    grad_y = cotangent.reshape(local_rows, features)
    block_row = block_order.reshape(-1)
    scale = 1.0 / math.sqrt(HEAD_DIM)
    line_rows = local_rows * line.size
    heads = HEADS // line.size
    sharing = line.size // KV_HEADS
    query_width = heads * HEAD_DIM
    bits_up = [1 << i for i in range(batch_size.bit_length() - 1)]
    bits_down = bits_up[::-1]
    owner_pairs = [
        (c * batch_size + b, b * ctx_size + c) for b in range(batch_size) for c in range(ctx_size)
    ]

    def slots(rows):
        return [
            rows[slot * local_rows : (slot + 1) * local_rows] for slot in range(line.size)
        ]

    def stack(parts):
        return jnp.concatenate(parts, axis=0)

    own_gains = jnp.stack((attn_gain, post_attn_gain, ffn_gain, post_ffn_gain))
    piece = own_gains.shape[1]
    spread = lax.dynamic_update_slice(
        jnp.zeros((4, devices, piece), BF16), own_gains[:, None], (0, flat_index, 0)
    )
    gains = everywhere(spread, line, batch_size, ("batch", "line", "pair")).reshape(4, features)
    gain_one, gain_two, gain_three, gain_four = gains[0], gains[1], gains[2], gains[3]

    weight_rows = query_weight.shape[0]

    def kv_targets(weight):
        return jnp.repeat(weight.reshape(weight_rows, KV_HEADS, HEAD_DIM), sharing, axis=1)

    def from_here(stacked):
        return lax.dynamic_slice_in_dim(
            jnp.concatenate((stacked, stacked), axis=0), line.at, line.size, axis=0
        )

    def from_start(turned):
        return lax.dynamic_slice_in_dim(
            jnp.concatenate((turned, turned), axis=0),
            (line.size - line.at) % line.size,
            line.size,
            axis=0,
        )

    per_target = jnp.concatenate(
        (
            query_weight.reshape(weight_rows, line.size, query_width),
            kv_targets(key_weight),
            kv_targets(value_weight),
        ),
        axis=2,
    )
    turned = from_here(jnp.transpose(per_target, (1, 0, 2)))
    received = [turned[0]] + [
        line.shift(turned[line.size - k], k) for k in range(1, line.size)
    ]
    batch_index = lax.axis_index("batch")
    even = line.parity == 0

    def placed(pieces, shape, block):
        whole = jnp.zeros(shape, BF16)
        for k, one in enumerate(pieces):
            other = line.partner(one)
            for parity, rows in ((line.parity, one), (1 - line.parity, other)):
                start, update = block(batch_index ^ k, parity, rows)
                whole = lax.dynamic_update_slice(whole, update, start)
        return whole

    w_half = from_start(jnp.stack(received))
    pieces = batch_pieces(w_half, batch_size)
    w_qkv = placed(
        pieces,
        (batch_size, line.size, 2) + w_half.shape[1:],
        lambda b, parity, rows: ((b, 0, parity, 0, 0), rows[None, :, None]),
    ).reshape(features, query_width + 2 * HEAD_DIM)

    out_half = lax.ppermute(out_weight, ("batch", "ctx"), owner_pairs)
    out_pieces = batch_pieces(out_half, batch_size)
    w_out = placed(
        out_pieces,
        (2, batch_size) + out_half.shape,
        lambda b, parity, rows: ((parity, b, 0, 0), rows[None, None]),
    ).reshape(-1, features)

    unit_rows = gate_weight.shape[0]
    gate_pieces = cube_gather(gate_weight, bits_up, batch_size)
    up_pieces = cube_gather(up_weight, bits_down, batch_size)
    down_pieces = cube_gather(down_weight, bits_up, batch_size)

    normed, inv_one = normalize(rows_x, gain_one)
    normed_in, _ = line.gather(normed.astype(BF16))
    qkv = stack([product(rows, w_qkv).astype(BF16) for rows in normed_in])
    own_kv = qkv[:, query_width:]
    kv = stack((own_kv, line.partner(own_kv)))
    keys = kv[:, :HEAD_DIM]
    values = kv[:, HEAD_DIM:]

    def by_head(rows):
        return stack([rows[:, h * HEAD_DIM : (h + 1) * HEAD_DIM] for h in range(heads)])

    def by_row(stacked):
        return jnp.concatenate(
            [stacked[h * line_rows : (h + 1) * line_rows] for h in range(heads)], axis=1
        )

    query = by_head(qkv[:, :query_width])

    def row_positions(blocks):
        inside = jnp.arange(local_rows, dtype=jnp.int32)
        return (blocks[:, None] * local_rows + inside[None, :]).reshape(-1)

    query_pos = row_positions(line.slot_blocks(block_row, line.parity))
    key_pos = jnp.concatenate(
        (query_pos, row_positions(line.slot_blocks(block_row, 1 - line.parity)))
    )
    visible = key_pos[None, :] <= jnp.tile(query_pos, heads)[:, None]
    tanh_val = jnp.tanh(rows_product(query, keys) * scale / SOFT_CAP)
    raw = jnp.where(visible, jnp.exp(SOFT_CAP * tanh_val), 0.0)
    totals = jnp.sum(raw, axis=1, keepdims=True)
    attended = (product(raw.astype(BF16), values) / totals).astype(BF16)
    attended_rows = by_row(attended)
    branch, _ = line.scatter(slots(product(attended_rows, w_out)))
    branch_normed, inv_two = normalize(branch, gain_two)
    middle = rows_x + branch_normed
    normed_m, inv_three = normalize(middle, gain_three)

    def with_partner(rows):
        return stack((rows, line.partner(rows)))

    def pair_sum(part):
        other = line.partner(part[local_rows:].astype(BF16))
        return part[:local_rows] + other.astype(F32)

    def expand(rows):
        both = with_partner(rows)
        gate_act = rows_product(both, w_gate)
        up_act = rows_product(both, w_up)
        return both, gate_act, up_act, geglu(gate_act, up_act).astype(BF16)

    def contract(forward):
        return pair_sum(product(forward[3], w_down))

    expanded, parts = [], []

    w_gate, w_up = stack(gate_pieces), stack(up_pieces)
    w_down = stack(down_pieces)

    def forward_work(k, arrived):
        expanded.append(expand(arrived[k - 1]))
        if k == line.size - 1:
            parts.extend(contract(forward) for forward in expanded[:-1])

    normed_rows, _ = line.gather(normed_m.astype(BF16), forward_work)
    expanded.append(expand(normed_rows[-1]))
    last = contract(expanded[-1])
    parts = parts + [contract(expanded[-2]), last]
    mid_rows = stack([e[0] for e in expanded])
    ffn_out, _ = line.scatter(parts)
    ffn_normed, inv_four = normalize(ffn_out, gain_four)
    output = middle + ffn_normed

    grad_ffn, grad_four = norm_back(ffn_out, inv_four, gain_four, grad_y)

    def shrink(rows, forward):
        both = with_partner(rows)
        _, pull_back = jax.vjp(geglu, forward[1], forward[2])
        gate_part, up_part = pull_back(rows_product(both, w_down))
        gate_part, up_part = gate_part.astype(BF16), up_part.astype(BF16)
        part = product(gate_part, w_gate) + product(up_part, w_up)
        return both, gate_part, up_part, pair_sum(part)

    ffn_rows, results = line.gather(
        grad_ffn.astype(BF16), lambda k, arrived: shrink(arrived[k - 1], expanded[k - 1])
    )
    shrunk = list(results) + [shrink(ffn_rows[-1], expanded[-1])]
    ffn_rows = stack([e[0] for e in shrunk])
    hidden = stack([e[3] for e in expanded])
    grad_gate = stack([e[1] for e in shrunk])
    grad_up = stack([e[2] for e in shrunk])

    def unit_grads(left, right, orders):
        total = cols_product(left, right).astype(BF16)
        ends = [unit_rows] if len(orders) == 1 else [unit_rows * 5 // 9, unit_rows]
        sums = []
        for start, end, bits in zip([0] + ends, ends, orders):
            pieces = [
                total[i * unit_rows + start : i * unit_rows + end] for i in cube_order(bits)
            ]
            sums.append((pieces, cube_send(pieces, bits[-1], batch_size), bits))
        return sums

    def first_sum(sums):
        after = []
        for pieces, sent, bits in sums:
            pieces, sent = cube_add(pieces, sent), None
            if len(bits) > 1:
                sent = cube_send(pieces, bits[-2], batch_size)
            after.append((pieces, sent, bits))
        return after

    def rest(sums):
        totals = []
        for pieces, sent, bits in sums:
            for bit in reversed(bits[:-1]):
                sent = cube_send(pieces, bit, batch_size) if sent is None else sent
                pieces, sent = cube_add(pieces, sent), None
            totals.append(pieces[0])
        return stack(totals) if len(totals) > 1 else totals[0]

    grad_nm, (down_sum, gate_sum, up_sum) = line.scatter(
        [e[3] for e in shrunk],
        (
            (functools.partial(unit_grads, orders=(bits_up,)), (hidden, ffn_rows)),
            (functools.partial(unit_grads, orders=(bits_down,)), (grad_gate, mid_rows)),
            (functools.partial(unit_grads, orders=(bits_up, bits_down)), (grad_up, mid_rows)),
        ),
    )

    grad_mid_part, grad_three = norm_back(middle, inv_three, gain_three, grad_nm)
    grad_mid = grad_y + grad_mid_part
    grad_branch, grad_two = norm_back(branch, inv_two, gain_two, grad_mid)
    gain_grads = jnp.stack((grad_two, grad_three, grad_four))

    gain_grads = everywhere(gain_grads, line, batch_size, ("line", "pair", "batch"))
    gain_grads = lax.dynamic_slice_in_dim(gain_grads, flat_index * piece, piece, axis=1)

    def back_work(k, arrived):
        if k == line.size - 2:
            return first_sum(down_sum)
        if k == line.size - 1:
            return first_sum(gate_sum), first_sum(up_sum)

    branch_rows, back_results = line.gather(grad_branch.astype(BF16), back_work)
    grad_branch_b = stack(branch_rows)
    down_grad = rest(back_results[-2])
    gate_grad = rest(back_results[-1][0])
    grad_att = by_head(rows_product(grad_branch_b, w_out).astype(BF16))
    delta = jnp.sum(grad_att.astype(F32) * attended.astype(F32), axis=1, keepdims=True)
    prob = raw / totals
    dprob = rows_product(grad_att, values)
    grad_z = (prob * (dprob - delta) * (1.0 - tanh_val * tanh_val) * scale).astype(BF16)
    grad_query = by_row(product(grad_z, keys).astype(BF16))
    grad_kv = jnp.concatenate(
        (cols_product(grad_z, query), cols_product(prob.astype(BF16), grad_att)), axis=1
    )
    grad_kv = grad_kv[:line_rows] + line.partner(grad_kv[line_rows:])
    grad_qkv = jnp.concatenate((grad_query, grad_kv.astype(BF16)), axis=1)

    def qkv_work(rows, grads):
        part = cols_product(rows, grads).astype(BF16).reshape(
            batch_size, line.size, 2, weight_rows, -1
        )
        part_even, part_odd = part[:, :, 0], part[:, :, 1]
        other = line.partner(jnp.where(even, part_odd, part_even))
        return jnp.where(even, part_even, part_odd), other

    pair_parts = []

    def qkv_first(rows, grads):
        pair_parts.extend(qkv_work(rows, grads))
        return ()

    def qkv_second():
        part = (pair_parts[0].astype(F32) + pair_parts[1].astype(F32)).astype(BF16)
        return part

    grad_in, (_, qkv_part) = line.scatter(
        slots(rows_product(grad_qkv, w_qkv)),
        ((qkv_first, (stack(normed_in), grad_qkv)), (qkv_second, ())),
    )
    qkv_part = batch_scatter(qkv_part, batch_index, batch_size)
    up_grad = rest(back_results[-1][1])

    out_part = cols_product(attended_rows, grad_branch_b).reshape(2, -1, features)
    out_other = line.partner(jnp.where(even, out_part[1], out_part[0]).astype(BF16))
    out_part = jnp.where(even, out_part[0], out_part[1]) + out_other.astype(F32)
    out_part = batch_scatter(
        out_part.astype(BF16).reshape(batch_size, -1, features), batch_index, batch_size
    )
    out_grad = lax.ppermute(
        out_part.astype(BF16),
        ("batch", "ctx"),
        [(there, here) for here, there in owner_pairs],
    ).astype(F32)

    turned = from_here(qkv_part.astype(BF16))
    returned = [turned[0]] + [
        line.shift(turned[line.size - k], k) for k in range(1, line.size)
    ]
    returned = from_start(jnp.stack(returned)).astype(F32)

    def columns(part):
        return jnp.transpose(part, (1, 0, 2)).reshape(weight_rows, -1)

    def kv_columns(part):
        part = part.reshape(KV_HEADS, sharing, weight_rows, HEAD_DIM)
        return columns(jnp.sum(part, axis=1))

    query_grad = columns(returned[:, :, :query_width])
    key_grad = kv_columns(returned[:, :, query_width : query_width + HEAD_DIM])
    value_grad = kv_columns(returned[:, :, query_width + HEAD_DIM :])

    grad_x_part, _ = norm_back(rows_x, inv_one, gain_one, grad_in)
    input_grad = grad_mid + grad_x_part
    attn_gain_grad = (
        jnp.sum(query_weight.astype(F32) * query_grad, axis=1)
        + jnp.sum(key_weight.astype(F32) * key_grad, axis=1)
        + jnp.sum(value_weight.astype(F32) * value_grad, axis=1)
    ) / attn_gain.astype(F32)
    return (
        output.reshape(1, local_rows, features),
        input_grad.reshape(1, local_rows, features),
        query_grad,
        key_grad,
        value_grad,
        out_grad,
        gate_grad,
        up_grad,
        down_grad,
        attn_gain_grad,
        gain_grads[0],
        gain_grads[1],
        gain_grads[2],
    )


def solution(mesh):
    sizes = (mesh.shape["batch"], mesh.shape["ctx"])
    rows = P("batch", "ctx", None)
    owned = P(("batch", "ctx"), None)
    vector = P(("batch", "ctx"))

    def program(*args):
        return on_device(sizes, *args)

    return jax.shard_map(
        program,
        mesh=mesh,
        in_specs=(rows, P("batch", None), rows) + (vector,) * 4 + (owned,) * 7,
        out_specs=(rows, rows) + (owned,) * 7 + (vector,) * 4,
        check_vma=False,
    )
```
